32 devices in a mesh: sym: 4 (over x, core), row: 8 (over z, y).
Axes of the slice: x: 2, y: 2, z: 4, core: 2. Of those that a mesh axis runs over, the one named last changes fastest.
Arguments:
- vectors: float32 [4, 32768, 256], P('sym', 'row'), may hold values from -6 to 6
- reflectors: float32 [4, 32768, 512], P('sym', 'row'), may hold values from -0.5 to 0.5
- factors: float32 [4, 4, 128, 128], P('sym'), may hold values from -0.03125 to 0.03125
- tiles: bfloat16 [4, 16, 512, 512], P('sym', 'row'), may hold values from -0.0029296875 to 0.0029296875
- tile_left: int32 [4, 16], P('sym', 'row'), may hold values from 0 to 7
- tile_right: int32 [4, 16], P('sym', 'row'), may hold values from 0 to 7
- tile_occupied_mask: int32 [4, 16], P('sym', 'row'), may hold values 0 or 1
- channels: int32 [4, 64], P('sym', 'row'), may hold values from 256 to 512
Outputs:
- dipole: float32 [4, 256, 256], P('sym', 'row')
The draws below stay inside these ranges and needn't reach their ends.
All inputs are finite; a program needn't handle non-finite values. No bound on the sum of `tile_occupied_mask` on one device may be relied on, other than what follows from the above.
Results may differ from the reference program's by a relative error of at most 0.0049.
Values may be sent and summed in bfloat16 or wider, within the bound.
A program may use at most 64 MiB of HBM per device.

```python
import jax
import jax.numpy as jnp
from jax import lax

EIG = 256
PANEL = 128
PANELS = 4
BLOCK = 512
TILE_SLOTS = 2
ORDER = 32768
SYMS = 4
BLOCKS_DEV = 8
BLOCKS = 64
TILES = 16


def set_ends(entries, rng, smallest, largest):
    extent = entries.shape
    place = [jax.random.randint(jax.random.fold_in(rng, axis), (), 0, extent[axis]) for axis in range(len(extent))]
    entries = entries.at[tuple(place)].set(smallest)
    longest = extent.index(max(extent))
    place[longest] = (place[longest] + 1) % extent[longest]
    return entries.at[tuple(place)].set(largest)


def levels(own_key, shape, shards, low, high):
    loudness = 1.0
    for dim, blocks in shards:
        heights = jax.random.uniform(jax.random.fold_in(jax.random.fold_in(own_key, 6), dim), (blocks,), jnp.float32, low / len(shards), high / len(shards))
        loudness = loudness * jnp.repeat(jnp.exp(heights), shape[dim] // blocks).reshape((-1,) + (1,) * (len(shape) - 1 - dim))
    return loudness


def bell_draw(rng, extent, scale, reach, cuts=(), held_as=jnp.bfloat16):
    drawn = scale * jax.random.normal(rng, extent, jnp.float32)
    if cuts:
        drawn = drawn * levels(rng, extent, cuts, -0.22, 0.18)
    return jnp.clip(drawn, -reach, reach).astype(held_as)


def setup_inputs(seed: int = 0) -> dict:
    key_of = jax.random.split(jax.random.key(seed), 9)
    vectors = bell_draw(key_of[0], (SYMS, ORDER, EIG), 1.0, 6.0, ((0, 4), (1, 8)), jnp.float32)
    reflectors = bell_draw(key_of[1], (SYMS, ORDER, PANELS * PANEL), PANEL ** -0.5, 0.5, ((0, 4), (1, 8)), jnp.float32)
    factors = bell_draw(key_of[2], (SYMS, PANELS, PANEL, PANEL), ORDER ** -0.5, 0.03125, ((0, 4),), jnp.float32)
    tiles = bell_draw(key_of[3], (SYMS, TILES, BLOCK, BLOCK), (BLOCK * BLOCK * TILES) ** -0.5, 0.0029296875, ((0, 4), (1, 8)))
    tile_left = set_ends(jax.random.randint(key_of[4], (SYMS, TILES), 0, BLOCKS_DEV), jax.random.fold_in(key_of[4], 1), 0, BLOCKS_DEV - 1).astype(jnp.int32)
    tile_right = set_ends(jax.random.randint(key_of[5], (SYMS, TILES), 0, BLOCKS_DEV), jax.random.fold_in(key_of[5], 1), 0, BLOCKS_DEV - 1).astype(jnp.int32)
    tile_occupied_mask = set_ends((jax.random.randint(key_of[6], (SYMS, TILES), 0, 4) < 3).astype(jnp.int32), jax.random.fold_in(key_of[6], 1), 0, 1)
    channels = set_ends(jax.random.randint(key_of[7], (SYMS, BLOCKS), BLOCK // 2, BLOCK + 1), jax.random.fold_in(key_of[7], 1), BLOCK // 2, BLOCK).astype(jnp.int32)
    return {"vectors": vectors, "reflectors": reflectors, "factors": factors, "tiles": tiles, "tile_left": tile_left, "tile_right": tile_right, "tile_occupied_mask": tile_occupied_mask, "channels": channels}


PRECISE = lax.Precision.HIGHEST


def back_transform(start, panels, factor_set):
    result = start
    for level in reversed(range(PANELS)):
        panel = panels[:, level * PANEL:(level + 1) * PANEL]
        inner_part = jnp.dot(panel.T, result, precision=PRECISE)
        result = result - jnp.dot(panel, jnp.dot(factor_set[level], inner_part, precision=PRECISE), precision=PRECISE)
    return result


def reference(vectors, reflectors, factors, tiles, tile_left, tile_right, tile_occupied_mask, channels):
    masked = []
    position = jnp.arange(BLOCK, dtype=jnp.int32)
    for symmetry_label in range(SYMS):
        result = back_transform(vectors[symmetry_label], reflectors[symmetry_label], factors[symmetry_label])
        keeper = (position[None, :] < channels[symmetry_label][:, None]).astype(jnp.float32)
        reshaped_block = result.reshape(BLOCKS, BLOCK, EIG) * keeper[:, :, None]
        masked.append(reshaped_block.astype(jnp.bfloat16))
    offsets = (jnp.arange(TILES, dtype=jnp.int32) // TILE_SLOTS) * BLOCKS_DEV
    dipole_output_list = []
    for symmetry_label in range(SYMS):
        paired_symmetry = (symmetry_label + 1) % SYMS
        bra_state_rows = masked[symmetry_label][(offsets + tile_left[symmetry_label]).astype(jnp.int32)]
        right_rows = masked[paired_symmetry][(offsets + tile_right[symmetry_label]).astype(jnp.int32)]
        bra_ket_product = jnp.einsum("tij,tjk->tik", tiles[symmetry_label].astype(jnp.float32), right_rows.astype(jnp.float32)).astype(jnp.bfloat16)
        tile_presence_mask = tile_occupied_mask[symmetry_label].astype(jnp.float32)
        dipole_output_list.append(jnp.einsum("agx,agh,a->xh", bra_state_rows.astype(jnp.float32), bra_ket_product.astype(jnp.float32), tile_presence_mask))
    return jnp.stack(dipole_output_list)
```

```python
import functools

import jax
import jax.numpy as jnp
from jax import lax
from jax.experimental import pallas as pl
from jax.experimental.pallas import tpu as pltpu
from jax.sharding import PartitionSpec as P

BLOCK = 512
F32 = jnp.float32
BF16 = jnp.bfloat16
MESH = pl.DeviceIdType.MESH


def split(value):
    high = value.astype(BF16)
    return high, (value - high.astype(F32)).astype(BF16)


def contract(first, second, dims):
    high, low = first
    other_high, other_low = second

    def dot(a, b):
        return lax.dot_general(a, b, (dims, ((), ())), preferred_element_type=F32)

    return dot(high, other_high) + (dot(high, other_low) + dot(low, other_high))


ROWS = ((0,), (0,))
PLAIN = ((1,), (0,))
COLUMNS = ((1,), (1,))


def coupled_ranges(first, count):
    if count < 2:
        return []
    half = count // 2
    here = [(first, half, first + half, count - half)]
    return here + coupled_ranges(first, half) + coupled_ranges(first + half, count - half)


def kernel(
    n,
    syms,
    x_hbm,
    v_hbm,
    f_ref,
    tiles_ref,
    right_ref,
    left_ref,
    occupied_ref,
    channels_ref,
    out_ref,
    x_buf,
    v_buf,
    v_high,
    v_low,
    slots_vmem,
    slots_smem,
    partial,
    landed,
    full,
    t_ref,
    u_high,
    u_low,
    ket_out,
    ket_in,
    own,
    dipole_out,
    dipole_in,
    x_sem,
    v_sem,
    slot_sem,
    reduce_send,
    reduce_recv,
    ket_send,
    ket_recv,
    dipole_send,
    dipole_recv,
):
    panels, width, _ = f_ref.shape
    blocks, _, eig = x_buf.shape
    tile_slots = tiles_ref.shape[0]
    steps = n.bit_length() - 1
    sym = lax.axis_index("sym")
    me = lax.axis_index("row")
    after = lax.rem(sym + 1, syms)
    before = lax.rem(sym + syms - 1, syms)

    def load(source, target, sems, r):
        return pltpu.make_async_copy(source.at[r], target.at[r], sems.at[r])

    for r in range(blocks):
        load(v_hbm, v_buf, v_sem, r).start()
    for r in range(blocks):
        load(x_hbm, x_buf, x_sem, r).start()

    barrier = pltpu.get_barrier_semaphore()
    for d in range(1, n):
        pl.semaphore_signal(
            barrier, inc=1, device_id=(sym, lax.rem(me + d, n)), device_id_type=MESH
        )
    for other in (after, before):
        pl.semaphore_signal(barrier, inc=1, device_id=(other, me), device_id_type=MESH)
    pl.semaphore_wait(barrier, n + 1)

    slots_copy = pltpu.make_async_remote_copy(
        src_ref=right_ref,
        dst_ref=slots_vmem,
        send_sem=slot_sem.at[0],
        recv_sem=slot_sem.at[1],
        device_id=(after, me),
        device_id_type=MESH,
    )
    slots_copy.start()

    ranges = coupled_ranges(0, panels)

    def couple(r, sums):
        load(v_hbm, v_buf, v_sem, r).wait()
        high, low = split(v_buf[r])
        v_high[r] = high
        v_low[r] = low
        out = []
        for total, (a, ca, b, cb) in zip(sums, ranges):
            pa = slice(a * width, (a + ca) * width)
            pb = slice(b * width, (b + cb) * width)
            out.append(
                total + contract((high[:, pa], low[:, pa]), (high[:, pb], low[:, pb]), ROWS)
            )
        return tuple(out)

    sums = lax.fori_loop(
        0, blocks, couple, tuple(jnp.zeros((ca * width, cb * width), F32) for _, ca, _, cb in ranges)
    )
    where = {}
    place = 0
    firsts = []
    for total, (a, ca, b, cb) in zip(sums, ranges):
        for i in range(ca):
            for j in range(cb):
                where[(a + i, b + j)] = place
                partial[place : place + width, :] = total[
                    i * width : (i + 1) * width, j * width : (j + 1) * width
                ]
                place = place + width
        firsts.append(place)
    coupled_rows = place
    jobs = [(0, firsts[0]), (firsts[0], coupled_rows - firsts[0])]
    group = panels // 2
    for begin in range(0, panels, group):
        jobs.append((coupled_rows + begin * eig, group * eig))

    copies = {}

    def offset_after(job, count):
        base, size = jobs[job]
        offset = base
        for b in range(count):
            offset = offset + lax.rem(me // (1 << b), 2) * (size >> (b + 1))
        return offset

    def aligned(offset, length):
        return pl.ds(pl.multiple_of(offset, 8), length)

    def start(job, phase):
        base, size = jobs[job]
        b = phase if phase < steps else 2 * steps - 1 - phase
        bit = lax.rem(me // (1 << b), 2)
        partner = me + (1 - 2 * bit) * (1 << b)
        half = size >> (b + 1)
        if phase < steps:
            source = partial.at[aligned(offset_after(job, b) + (1 - bit) * half, half)]
            slot = base + size - 2 * half
            target = landed.at[slot : slot + half]
        else:
            span = aligned(offset_after(job, b + 1), half)
            source = full.at[span]
            target = full.at[span]
        copy = pltpu.make_async_remote_copy(
            src_ref=source,
            dst_ref=target,
            send_sem=reduce_send.at[job, phase],
            recv_sem=reduce_recv.at[job, phase],
            device_id=(sym, partner),
            device_id_type=MESH,
        )
        copy.start()
        copies[(job, phase)] = copy

    def finish(job, phase):
        base, size = jobs[job]
        copies[(job, phase)].wait()
        if phase < steps:
            half = size >> (phase + 1)
            span = aligned(offset_after(job, phase + 1), half)
            slot = base + size - 2 * half
            target = full if phase == steps - 1 else partial
            target[span, :] = partial[span, :] + landed[slot : slot + half, :]
        if phase + 1 < 2 * steps:
            start(job, phase + 1)

    start(0, 0)
    start(1, 0)

    def project(r, total):
        load(x_hbm, x_buf, x_sem, r).wait()
        return total + contract(split(x_buf[r]), (v_high[r], v_low[r]), ROWS)

    projected = lax.fori_loop(0, blocks, project, jnp.zeros((eig, panels * width), F32))
    for k in range(panels):
        at = coupled_rows + k * eig
        partial[at : at + eig, :] = projected[:, k * width : (k + 1) * width]
    for job in range(2, len(jobs)):
        start(job, 0)

    slots_copy.wait()
    to_smem = pltpu.make_async_copy(slots_vmem, slots_smem, slot_sem.at[2])
    to_smem.start()

    def transfer_matrix():
        for k in reversed(range(panels)):
            here = slice(k * width, (k + 1) * width)
            t_ref[here, here] = f_ref[k]
            if k:
                t_ref[here, : k * width] = jnp.zeros((width, k * width), F32)
            if k < panels - 1:
                later = slice((k + 1) * width, panels * width)
                row = jnp.concatenate(
                    [full[where[(k, j)] : where[(k, j)] + width, :] for j in range(k + 1, panels)],
                    axis=1,
                )
                inner = contract(split(row), split(t_ref[later, later]), PLAIN)
                t_ref[here, later] = -contract(split(f_ref[k]), split(inner), PLAIN)

    for wave in range(2 * steps + len(jobs) - 1):
        for job in range(len(jobs)):
            phase = wave - job
            if 0 <= phase < 2 * steps:
                finish(job, phase)
                if job == 1 and phase == 2 * steps - 1:
                    transfer_matrix()

    gathered = jnp.concatenate(
        [full[coupled_rows + k * eig : coupled_rows + (k + 1) * eig, :] for k in range(panels)],
        axis=1,
    )
    high, low = split(contract(split(t_ref[...]), split(gathered), COLUMNS))
    u_high[...] = high
    u_low[...] = low

    def finished(slot):
        change = contract((v_high[slot], v_low[slot]), (u_high[...], u_low[...]), PLAIN)
        live = lax.broadcasted_iota(jnp.int32, (BLOCK, eig), 0) < channels_ref[0, slot]
        return jnp.where(live, x_buf[slot] - change, 0.0)

    to_smem.wait()
    kets = []
    for t in range(tile_slots):
        ket_out[t] = finished(slots_smem[0, t]).astype(BF16)
        copy = pltpu.make_async_remote_copy(
            src_ref=ket_out.at[t],
            dst_ref=ket_in.at[t],
            send_sem=ket_send.at[t],
            recv_sem=ket_recv.at[t],
            device_id=(before, me),
            device_id_type=MESH,
        )
        copy.start()
        kets.append(copy)
    bras = []
    for t in range(tile_slots):
        occupied = occupied_ref[0, t].astype(F32)
        bras.append((finished(left_ref[0, t]) * occupied).astype(BF16))
    total = jnp.zeros((eig, eig), F32)
    for t in range(tile_slots):
        kets[t].wait()
        product = jnp.dot(tiles_ref[t], ket_in[t], preferred_element_type=F32).astype(BF16)
        total = total + lax.dot_general(
            bras[t], product, (ROWS, ((), ())), preferred_element_type=F32
        )
    share = eig // n
    own[...] = total.reshape(n, share, eig)
    dipole_out[...] = total.reshape(n, share, eig).astype(BF16)
    sends = []
    for d in range(1, n):
        target = lax.rem(me + d, n)
        copy = pltpu.make_async_remote_copy(
            src_ref=dipole_out.at[target],
            dst_ref=dipole_in.at[d - 1],
            send_sem=dipole_send.at[d - 1],
            recv_sem=dipole_recv.at[d - 1],
            device_id=(sym, target),
            device_id_type=MESH,
        )
        copy.start()
        sends.append(copy)
    result = own[me]
    for d in range(1, n):
        sends[d - 1].wait()
        result = result + dipole_in[d - 1].astype(F32)
    out_ref[0] = result


def on_device(
    n,
    syms,
    vectors,
    reflectors,
    factors,
    tiles,
    tile_left,
    tile_right,
    tile_occupied_mask,
    channels,
):
    start = vectors[0]
    panels = reflectors[0]
    rows, eig = start.shape
    count, width, _ = factors.shape[1:]
    tile_slots = tiles.shape[1]
    steps = n.bit_length() - 1
    blocks = rows // BLOCK
    coupled_rows = count * (count - 1) // 2 * width
    reduced = coupled_rows + count * eig
    share = eig // n
    dma = pltpu.SemaphoreType.DMA
    vmem = pl.BlockSpec(memory_space=pltpu.VMEM)
    smem = pl.BlockSpec(memory_space=pltpu.SMEM)
    hbm = pl.BlockSpec(memory_space=pl.ANY)
    return pl.pallas_call(
        functools.partial(kernel, n, syms),
        out_shape=jax.ShapeDtypeStruct((1, share, eig), F32),
        in_specs=[hbm, hbm, vmem, vmem, vmem, smem, smem, smem],
        out_specs=vmem,
        scratch_shapes=[
            pltpu.VMEM((blocks, BLOCK, eig), F32),
            pltpu.VMEM((blocks, BLOCK, count * width), F32),
            pltpu.VMEM((blocks, BLOCK, count * width), BF16),
            pltpu.VMEM((blocks, BLOCK, count * width), BF16),
            pltpu.VMEM((1, tile_slots), jnp.int32),
            pltpu.SMEM((1, tile_slots), jnp.int32),
            pltpu.VMEM((reduced, width), F32),
            pltpu.VMEM((reduced, width), F32),
            pltpu.VMEM((reduced, width), F32),
            pltpu.VMEM((count * width, count * width), F32),
            pltpu.VMEM((count * width, eig), BF16),
            pltpu.VMEM((count * width, eig), BF16),
            pltpu.VMEM((tile_slots, BLOCK, eig), BF16),
            pltpu.VMEM((tile_slots, BLOCK, eig), BF16),
            pltpu.VMEM((n, share, eig), F32),
            pltpu.VMEM((n, share, eig), BF16),
            pltpu.VMEM((n - 1, share, eig), BF16),
            dma((blocks,)),
            dma((blocks,)),
            dma((3,)),
            dma((4, 2 * steps)),
            dma((4, 2 * steps)),
            dma((tile_slots,)),
            dma((tile_slots,)),
            dma((n - 1,)),
            dma((n - 1,)),
        ],
        compiler_params=pltpu.CompilerParams(
            collective_id=0, has_side_effects=True, vmem_limit_bytes=60 * 1024 * 1024
        ),
    )(
        start.reshape(blocks, BLOCK, eig),
        panels.reshape(blocks, BLOCK, count * width),
        factors[0],
        tiles[0],
        tile_right,
        tile_left,
        tile_occupied_mask,
        channels,
    )


def solution(mesh):
    return jax.shard_map(
        functools.partial(on_device, mesh.shape["row"], mesh.shape["sym"]),
        mesh=mesh,
        in_specs=(
            P("sym", "row", None),
            P("sym", "row", None),
            P("sym", None, None, None),
            P("sym", "row", None, None),
            P("sym", "row"),
            P("sym", "row"),
            P("sym", "row"),
            P("sym", "row"),
        ),
        out_specs=P("sym", "row", None),
        check_vma=False,
    )
```

```python
import functools

import jax
import jax.numpy as jnp
from jax import lax
from jax.experimental import pallas as pl
from jax.experimental.pallas import tpu as pltpu
from jax.sharding import PartitionSpec as P

BLOCK = 512
LANES = 128
JOB_ROWS = 256
SKEW = 3
F32 = jnp.float32
BF16 = jnp.bfloat16
MESH = pl.DeviceIdType.MESH


def split(value):
    high = value.astype(BF16)
    return high, (value - high.astype(F32)).astype(BF16)


def contract(first, second, dims):
    high, low = first
    other_high, other_low = second

    def dot(a, b):
        return lax.dot_general(a, b, (dims, ((), ())), preferred_element_type=F32)

    return dot(high, other_high) + (dot(high, other_low) + dot(low, other_high))


ROWS = ((0,), (0,))
PLAIN = ((1,), (0,))
COLUMNS = ((1,), (1,))


def coupled_ranges(first, count):
    if count < 2:
        return []
    half = count // 2
    here = [(first, half, first + half, count - half)]
    return here + coupled_ranges(first, half) + coupled_ranges(first + half, count - half)


def radices(n):
    bits = n.bit_length() - 1
    return [2] * (bits % 2) + [4] * (bits // 2)


def kernel(
    n,
    syms,
    x_hbm,
    v_hbm,
    f_ref,
    tiles_ref,
    right_ref,
    left_ref,
    occupied_ref,
    channels_ref,
    out_ref,
    x_buf,
    v_buf,
    v_high,
    v_low,
    slots_vmem,
    slots_smem,
    partial,
    landed,
    full,
    t_ref,
    u_high,
    u_low,
    ket_out,
    ket_in,
    bras,
    own,
    dipole_out,
    dipole_in,
    x_sem,
    v_sem,
    slot_sem,
    reduce_send,
    reduce_recv,
    ket_send,
    ket_recv,
    dipole_send,
    dipole_recv,
):
    panels, width, _ = f_ref.shape
    blocks, _, eig = x_buf.shape
    tile_slots = tiles_ref.shape[0]
    halves = eig // LANES
    sym = lax.axis_index("sym")
    me = lax.axis_index("row")
    after = lax.rem(sym + 1, syms)
    before = lax.rem(sym + syms - 1, syms)

    def load(source, target, sems, r):
        return pltpu.make_async_copy(source.at[r], target.at[r], sems.at[r])

    for r in range(blocks):
        load(v_hbm, v_buf, v_sem, r).start()
    for r in range(blocks):
        load(x_hbm, x_buf, x_sem, r).start()

    barrier = pltpu.get_barrier_semaphore()
    for d in range(1, n):
        pl.semaphore_signal(
            barrier, inc=1, device_id=(sym, lax.rem(me + d, n)), device_id_type=MESH
        )
    for other in (after, before):
        pl.semaphore_signal(barrier, inc=1, device_id=(other, me), device_id_type=MESH)
    pl.semaphore_wait(barrier, n + 1)

    slots_copy = pltpu.make_async_remote_copy(
        src_ref=right_ref,
        dst_ref=slots_vmem,
        send_sem=slot_sem.at[0],
        recv_sem=slot_sem.at[1],
        device_id=(after, me),
        device_id_type=MESH,
    )
    slots_copy.start()

    ranges = coupled_ranges(0, panels)

    def couple(r, sums):
        load(v_hbm, v_buf, v_sem, r).wait()
        high, low = split(v_buf[r])
        v_high[r] = high
        v_low[r] = low
        out = []
        for total, (a, ca, b, cb) in zip(sums, ranges):
            pa = slice(a * width, (a + ca) * width)
            pb = slice(b * width, (b + cb) * width)
            out.append(
                total + contract((high[:, pa], low[:, pa]), (high[:, pb], low[:, pb]), ROWS)
            )
        return tuple(out)

    sums = lax.fori_loop(
        0, blocks, couple, tuple(jnp.zeros((ca * width, cb * width), F32) for _, ca, _, cb in ranges)
    )
    where = {}
    place = 0
    for total, (a, ca, b, cb) in zip(sums, ranges):
        for i in range(ca):
            for j in range(cb):
                where[(a + i, b + j)] = place
                partial[place : place + width, :] = total[
                    i * width : (i + 1) * width, j * width : (j + 1) * width
                ]
                place = place + width
    coupled_rows = place
    total_rows = coupled_rows + panels * eig
    job_rows = max(JOB_ROWS, 8 * n)
    job_count = total_rows // job_rows
    coupled_jobs = coupled_rows // job_rows
    jobs_of_half = (job_count - coupled_jobs) // halves

    copies = {}
    factors = radices(n)
    levels = len(factors)
    strides = [1]
    sizes = [job_rows]
    for radix in factors:
        strides.append(strides[-1] * radix)
        sizes.append(sizes[-1] // radix)
    slots = [0]
    for radix, size in zip(factors, sizes[1:]):
        slots.append(slots[-1] + (radix - 1) * size)

    def digit(level):
        return lax.rem(me // strides[level], factors[level])

    def span_after(job, level, last=None):
        offset = job * job_rows
        for below in range(level):
            place = digit(below) if last is None or below < level - 1 else last
            offset = offset + place * sizes[below + 1]
        return pl.ds(pl.multiple_of(offset, 8), sizes[level])

    def start(job, phase):
        level = phase if phase < levels else 2 * levels - 1 - phase
        radix = factors[level]
        piece = sizes[level + 1]
        copies[(job, phase)] = []
        for k in range(1, radix):
            other = lax.rem(digit(level) + k, radix)
            if phase < levels:
                source = partial.at[span_after(job, level + 1, other)]
                slot = job * job_rows + slots[level] + (k - 1) * piece
                target = landed.at[slot : slot + piece]
            else:
                source = full.at[span_after(job, level + 1)]
                target = source
            copy = pltpu.make_async_remote_copy(
                src_ref=source,
                dst_ref=target,
                send_sem=reduce_send.at[job, phase, k - 1],
                recv_sem=reduce_recv.at[job, phase, k - 1],
                device_id=(sym, me + (other - digit(level)) * strides[level]),
                device_id_type=MESH,
            )
            copy.start()
            copies[(job, phase)].append(copy)

    def finish(job, phase):
        for copy in copies[(job, phase)]:
            copy.wait()
        if phase < levels:
            piece = sizes[phase + 1]
            span = span_after(job, phase + 1)
            value = partial[span, :]
            for k in range(1, factors[phase]):
                slot = job * job_rows + slots[phase] + (k - 1) * piece
                value = value + landed[slot : slot + piece, :]
            target = full if phase == levels - 1 else partial
            target[span, :] = value
        if phase + 1 < 2 * levels:
            start(job, phase + 1)

    for job in range(coupled_jobs):
        start(job, 0)

    def project(r, total):
        load(x_hbm, x_buf, x_sem, r).wait()
        return total + contract(split(x_buf[r]), (v_high[r], v_low[r]), ROWS)

    projected = lax.fori_loop(0, blocks, project, jnp.zeros((eig, panels * width), F32))
    for h in range(halves):
        for k in range(panels):
            at = coupled_rows + (h * panels + k) * LANES
            partial[at : at + LANES, :] = projected[
                h * LANES : (h + 1) * LANES, k * width : (k + 1) * width
            ]
    for job in range(coupled_jobs, job_count):
        start(job, 0)

    slots_copy.wait()
    to_smem = pltpu.make_async_copy(slots_vmem, slots_smem, slot_sem.at[2])
    to_smem.start()

    def transfer_matrix():
        for k in reversed(range(panels)):
            here = slice(k * width, (k + 1) * width)
            t_ref[here, here] = f_ref[k]
            if k:
                t_ref[here, : k * width] = jnp.zeros((width, k * width), F32)
            if k < panels - 1:
                later = slice((k + 1) * width, panels * width)
                row = jnp.concatenate(
                    [full[where[(k, j)] : where[(k, j)] + width, :] for j in range(k + 1, panels)],
                    axis=1,
                )
                inner = contract(split(row), split(t_ref[later, later]), PLAIN)
                t_ref[here, later] = -contract(split(f_ref[k]), split(inner), PLAIN)

    def update(h):
        begin = coupled_rows + h * panels * LANES
        gathered = jnp.concatenate(
            [full[begin + k * LANES : begin + (k + 1) * LANES, :] for k in range(panels)], axis=1
        )
        high, low = split(contract(split(t_ref[...]), split(gathered), COLUMNS))
        u_high[h] = high
        u_low[h] = low

    def finished(slot, h):
        change = contract((v_high[slot], v_low[slot]), (u_high[h], u_low[h]), PLAIN)
        live = lax.broadcasted_iota(jnp.int32, (BLOCK, LANES), 0) < channels_ref[0, slot]
        value = x_buf[slot, :, h * LANES : (h + 1) * LANES] - change
        return jnp.where(live, value, 0.0)

    kets = {}

    def right_blocks(h):
        for t in range(tile_slots):
            ket_out[h, t] = finished(slots_smem[0, t], h).astype(BF16)
            copy = pltpu.make_async_remote_copy(
                src_ref=ket_out.at[h, t],
                dst_ref=ket_in.at[h, t],
                send_sem=ket_send.at[h, t],
                recv_sem=ket_recv.at[h, t],
                device_id=(before, me),
                device_id_type=MESH,
            )
            copy.start()
            kets[(h, t)] = copy

    def left_blocks(h):
        for t in range(tile_slots):
            occupied = occupied_ref[0, t].astype(F32)
            bras[t, :, h * LANES : (h + 1) * LANES] = (
                finished(left_ref[0, t], h) * occupied
            ).astype(BF16)

    to_smem.wait()
    events = [(job + SKEW * phase, job, phase) for job in range(job_count) for phase in range(2 * levels)]
    for _, job, phase in sorted(events):
        finish(job, phase)
        if phase == 2 * levels - 1:
            if job == coupled_jobs - 1:
                transfer_matrix()
            done = job + 1 - coupled_jobs
            if done > 0 and done % jobs_of_half == 0:
                h = done // jobs_of_half - 1
                update(h)
                right_blocks(h)
                if h < halves - 1:
                    left_blocks(h)
    left_blocks(halves - 1)

    share = eig // n
    sends = []
    for h in range(halves):
        total = jnp.zeros((eig, LANES), F32)
        for t in range(tile_slots):
            kets[(h, t)].wait()
            product = jnp.dot(tiles_ref[t], ket_in[h, t], preferred_element_type=F32).astype(BF16)
            total = total + lax.dot_general(
                bras[t], product, (ROWS, ((), ())), preferred_element_type=F32
            )
        own[h] = total.reshape(n, share, LANES)
        dipole_out[h] = total.reshape(n, share, LANES).astype(BF16)
        for d in range(1, n):
            target = lax.rem(me + d, n)
            copy = pltpu.make_async_remote_copy(
                src_ref=dipole_out.at[h, target],
                dst_ref=dipole_in.at[h, d - 1],
                send_sem=dipole_send.at[h, d - 1],
                recv_sem=dipole_recv.at[h, d - 1],
                device_id=(sym, target),
                device_id_type=MESH,
            )
            copy.start()
            sends.append((h, d, copy))
    results = [own[h, me] for h in range(halves)]
    for h, d, copy in sends:
        copy.wait()
        results[h] = results[h] + dipole_in[h, d - 1].astype(F32)
    for h in range(halves):
        out_ref[0, :, h * LANES : (h + 1) * LANES] = results[h]


def on_device(
    n,
    syms,
    vectors,
    reflectors,
    factors,
    tiles,
    tile_left,
    tile_right,
    tile_occupied_mask,
    channels,
):
    start = vectors[0]
    panels = reflectors[0]
    rows, eig = start.shape
    count, width, _ = factors.shape[1:]
    tile_slots = tiles.shape[1]
    halves = eig // LANES
    phases = 2 * len(radices(n))
    peers = max(radices(n)) - 1
    blocks = rows // BLOCK
    coupled_rows = count * (count - 1) // 2 * width
    reduced = coupled_rows + count * eig
    jobs = reduced // max(JOB_ROWS, 8 * n)
    share = eig // n
    dma = pltpu.SemaphoreType.DMA
    vmem = pl.BlockSpec(memory_space=pltpu.VMEM)
    smem = pl.BlockSpec(memory_space=pltpu.SMEM)
    hbm = pl.BlockSpec(memory_space=pl.ANY)
    return pl.pallas_call(
        functools.partial(kernel, n, syms),
        out_shape=jax.ShapeDtypeStruct((1, share, eig), F32),
        in_specs=[hbm, hbm, vmem, vmem, vmem, smem, smem, smem],
        out_specs=vmem,
        scratch_shapes=[
            pltpu.VMEM((blocks, BLOCK, eig), F32),
            pltpu.VMEM((blocks, BLOCK, count * width), F32),
            pltpu.VMEM((blocks, BLOCK, count * width), BF16),
            pltpu.VMEM((blocks, BLOCK, count * width), BF16),
            pltpu.VMEM((1, tile_slots), jnp.int32),
            pltpu.SMEM((1, tile_slots), jnp.int32),
            pltpu.VMEM((reduced, width), F32),
            pltpu.VMEM((reduced, width), F32),
            pltpu.VMEM((reduced, width), F32),
            pltpu.VMEM((count * width, count * width), F32),
            pltpu.VMEM((halves, count * width, LANES), BF16),
            pltpu.VMEM((halves, count * width, LANES), BF16),
            pltpu.VMEM((halves, tile_slots, BLOCK, LANES), BF16),
            pltpu.VMEM((halves, tile_slots, BLOCK, LANES), BF16),
            pltpu.VMEM((tile_slots, BLOCK, eig), BF16),
            pltpu.VMEM((halves, n, share, LANES), F32),
            pltpu.VMEM((halves, n, share, LANES), BF16),
            pltpu.VMEM((halves, n - 1, share, LANES), BF16),
            dma((blocks,)),
            dma((blocks,)),
            dma((3,)),
            dma((jobs, phases, peers)),
            dma((jobs, phases, peers)),
            dma((halves, tile_slots)),
            dma((halves, tile_slots)),
            dma((halves, n - 1)),
            dma((halves, n - 1)),
        ],
        compiler_params=pltpu.CompilerParams(
            collective_id=0, has_side_effects=True, vmem_limit_bytes=60 * 1024 * 1024
        ),
    )(
        start.reshape(blocks, BLOCK, eig),
        panels.reshape(blocks, BLOCK, count * width),
        factors[0],
        tiles[0],
        tile_right,
        tile_left,
        tile_occupied_mask,
        channels,
    )


def solution(mesh):
    return jax.shard_map(
        functools.partial(on_device, mesh.shape["row"], mesh.shape["sym"]),
        mesh=mesh,
        in_specs=(
            P("sym", "row", None),
            P("sym", "row", None),
            P("sym", None, None, None),
            P("sym", "row", None, None),
            P("sym", "row"),
            P("sym", "row"),
            P("sym", "row"),
            P("sym", "row"),
        ),
        out_specs=P("sym", "row", None),
        check_vma=False,
    )
```

```python
import functools

import jax
import jax.numpy as jnp
from jax import lax
from jax.experimental import pallas as pl
from jax.experimental.pallas import tpu as pltpu
from jax.sharding import PartitionSpec as P

BLOCK = 512
LANES = 128
JOB_ROWS = 256
SKEW = 3
SWAPPED = (1, 3, 5)
EARLY = ((), ((0, 0),), ((1, 0),))
F32 = jnp.float32
BF16 = jnp.bfloat16
MESH = pl.DeviceIdType.MESH


def split(value):
    high = value.astype(BF16)
    return high, (value - high.astype(F32)).astype(BF16)


def contract(first, second, dims):
    high, low = first
    other_high, other_low = second

    def dot(a, b):
        return lax.dot_general(a, b, (dims, ((), ())), preferred_element_type=F32)

    return dot(high, other_high) + (dot(high, other_low) + dot(low, other_high))


ROWS = ((0,), (0,))
PLAIN = ((1,), (0,))
COLUMNS = ((1,), (1,))


def coupled_ranges(first, count):
    if count < 2:
        return []
    half = count // 2
    here = [(first, half, first + half, count - half)]
    return here + coupled_ranges(first, half) + coupled_ranges(first + half, count - half)


def exchanges(n, job):
    strides = [1 << bit for bit in range(n.bit_length() - 1)]
    if job in SWAPPED and len(strides) > 1:
        strides[:2] = strides[1::-1]
    return strides


def kernel(
    n,
    syms,
    x_hbm,
    v_hbm,
    f_hbm,
    tiles_hbm,
    right_ref,
    left_ref,
    occupied_ref,
    channels_ref,
    out_ref,
    x_buf,
    v_buf,
    v_high,
    v_low,
    slots_vmem,
    slots_smem,
    partial,
    landed,
    full,
    t_ref,
    u_high,
    u_low,
    ket_out,
    ket_in,
    bras,
    own,
    dipole_out,
    dipole_in,
    f_ref,
    tiles_ref,
    x_sem,
    v_sem,
    slot_sem,
    operand_sem,
    reduce_send,
    reduce_recv,
    ket_send,
    ket_recv,
    dipole_send,
    dipole_recv,
):
    panels, width, _ = f_ref.shape
    blocks, _, eig = x_buf.shape
    tile_slots = tiles_ref.shape[0]
    halves = eig // LANES
    sym = lax.axis_index("sym")
    me = lax.axis_index("row")
    after = lax.rem(sym + 1, syms)
    before = lax.rem(sym + syms - 1, syms)

    def load(source, target, sems, r):
        return pltpu.make_async_copy(source.at[r], target.at[r], sems.at[r])

    for r in range(blocks):
        load(v_hbm, v_buf, v_sem, r).start()
    for r in range(blocks):
        load(x_hbm, x_buf, x_sem, r).start()

    f_copy = pltpu.make_async_copy(f_hbm, f_ref, operand_sem.at[0])
    f_copy.start()
    tiles_copy = pltpu.make_async_copy(tiles_hbm, tiles_ref, operand_sem.at[1])
    tiles_copy.start()

    barrier = pltpu.get_barrier_semaphore()
    for d in range(1, n):
        pl.semaphore_signal(
            barrier, inc=1, device_id=(sym, lax.rem(me + d, n)), device_id_type=MESH
        )
    for other in (after, before):
        pl.semaphore_signal(barrier, inc=1, device_id=(other, me), device_id_type=MESH)
    pl.semaphore_wait(barrier, n + 1)

    slots_copy = pltpu.make_async_remote_copy(
        src_ref=right_ref,
        dst_ref=slots_vmem,
        send_sem=slot_sem.at[0],
        recv_sem=slot_sem.at[1],
        device_id=(after, me),
        device_id_type=MESH,
    )
    slots_copy.start()

    ranges = coupled_ranges(0, panels)

    def couple(r, sums):
        load(v_hbm, v_buf, v_sem, r).wait()
        high, low = split(v_buf[r])
        v_high[r] = high
        v_low[r] = low
        out = []
        for total, (a, ca, b, cb) in zip(sums, ranges):
            pa = slice(a * width, (a + ca) * width)
            pb = slice(b * width, (b + cb) * width)
            out.append(
                total + contract((high[:, pa], low[:, pa]), (high[:, pb], low[:, pb]), ROWS)
            )
        return tuple(out)

    sums = lax.fori_loop(
        0, blocks, couple, tuple(jnp.zeros((ca * width, cb * width), F32) for _, ca, _, cb in ranges)
    )
    where = {}
    place = 0
    for total, (a, ca, b, cb) in zip(sums, ranges):
        for i in range(ca):
            for j in range(cb):
                where[(a + i, b + j)] = place
                partial[place : place + width, :] = total[
                    i * width : (i + 1) * width, j * width : (j + 1) * width
                ]
                place = place + width
    coupled_rows = place
    total_rows = coupled_rows + panels * eig
    job_rows = max(JOB_ROWS, 8 * n)
    job_count = total_rows // job_rows
    coupled_jobs = coupled_rows // job_rows
    jobs_of_half = (job_count - coupled_jobs) // halves

    copies = {}
    levels = n.bit_length() - 1

    def digit(job, level):
        return lax.rem(me // exchanges(n, job)[level], 2)

    def span_after(job, level, flip=False):
        offset = job * job_rows
        for below in range(level):
            place = digit(job, below)
            if flip and below == level - 1:
                place = 1 - place
            offset = offset + place * (job_rows >> (below + 1))
        return pl.ds(pl.multiple_of(offset, 8), job_rows >> level)

    def landing(job, level):
        piece = job_rows >> (level + 1)
        slot = (job + 1) * job_rows - 2 * piece
        return slice(slot, slot + piece)

    def start(job, phase):
        level = phase if phase < levels else 2 * levels - 1 - phase
        if phase < levels:
            source = partial.at[span_after(job, level + 1, True)]
            target = landed.at[landing(job, level)]
        else:
            source = full.at[span_after(job, level + 1)]
            target = source
        partner = me + (1 - 2 * digit(job, level)) * exchanges(n, job)[level]
        copy = pltpu.make_async_remote_copy(
            src_ref=source,
            dst_ref=target,
            send_sem=reduce_send.at[job, phase],
            recv_sem=reduce_recv.at[job, phase],
            device_id=(sym, partner),
            device_id_type=MESH,
        )
        copy.start()
        copies[(job, phase)] = copy

    def finish(job, phase):
        copies[(job, phase)].wait()
        if phase < levels:
            span = span_after(job, phase + 1)
            target = full if phase == levels - 1 else partial
            target[span, :] = partial[span, :] + landed[landing(job, phase), :]
        if phase + 1 < 2 * levels:
            start(job, phase + 1)

    for job in range(coupled_jobs):
        start(job, 0)

    def project(r, total):
        load(x_hbm, x_buf, x_sem, r).wait()
        return total + contract(split(x_buf[r]), (v_high[r], v_low[r]), ROWS)

    projected = jnp.zeros((eig, panels * width), F32)
    parts = len(EARLY) + 1
    for part in range(parts):
        projected = lax.fori_loop(
            part * blocks // parts, (part + 1) * blocks // parts, project, projected
        )
        if part < parts - 1:
            for job, phase in EARLY[part]:
                finish(job, phase)
    for h in range(halves):
        for k in range(panels):
            at = coupled_rows + (h * panels + k) * LANES
            partial[at : at + LANES, :] = projected[
                h * LANES : (h + 1) * LANES, k * width : (k + 1) * width
            ]
    for job in range(coupled_jobs, job_count):
        start(job, 0)

    slots_copy.wait()
    to_smem = pltpu.make_async_copy(slots_vmem, slots_smem, slot_sem.at[2])
    to_smem.start()

    def transfer_matrix():
        f_copy.wait()
        for k in reversed(range(panels)):
            here = slice(k * width, (k + 1) * width)
            t_ref[here, here] = f_ref[k]
            if k:
                t_ref[here, : k * width] = jnp.zeros((width, k * width), F32)
            if k < panels - 1:
                later = slice((k + 1) * width, panels * width)
                row = jnp.concatenate(
                    [full[where[(k, j)] : where[(k, j)] + width, :] for j in range(k + 1, panels)],
                    axis=1,
                )
                inner = contract(split(row), split(t_ref[later, later]), PLAIN)
                t_ref[here, later] = -contract(split(f_ref[k]), split(inner), PLAIN)

    def update(h):
        begin = coupled_rows + h * panels * LANES
        gathered = jnp.concatenate(
            [full[begin + k * LANES : begin + (k + 1) * LANES, :] for k in range(panels)], axis=1
        )
        high, low = split(contract(split(t_ref[...]), split(gathered), COLUMNS))
        u_high[h] = high
        u_low[h] = low

    def finished(slot, h):
        change = contract((v_high[slot], v_low[slot]), (u_high[h], u_low[h]), PLAIN)
        live = lax.broadcasted_iota(jnp.int32, (BLOCK, LANES), 0) < channels_ref[0, slot]
        value = x_buf[slot, :, h * LANES : (h + 1) * LANES] - change
        return jnp.where(live, value, 0.0)

    kets = {}

    def right_blocks(h):
        for t in range(tile_slots):
            ket_out[h, t] = finished(slots_smem[0, t], h).astype(BF16)
            copy = pltpu.make_async_remote_copy(
                src_ref=ket_out.at[h, t],
                dst_ref=ket_in.at[h, t],
                send_sem=ket_send.at[h, t],
                recv_sem=ket_recv.at[h, t],
                device_id=(before, me),
                device_id_type=MESH,
            )
            copy.start()
            kets[(h, t)] = copy

    def left_blocks(h):
        for t in range(tile_slots):
            occupied = occupied_ref[0, t].astype(F32)
            bras[t, :, h * LANES : (h + 1) * LANES] = (
                finished(left_ref[0, t], h) * occupied
            ).astype(BF16)

    to_smem.wait()
    events = [(job + SKEW * phase, job, phase) for job in range(job_count) for phase in range(2 * levels)]
    early = [event for part in EARLY for event in part]
    for _, job, phase in sorted(events):
        if (job, phase) not in early:
            finish(job, phase)
        if phase == 2 * levels - 1:
            if job == coupled_jobs - 1:
                transfer_matrix()
            done = job + 1 - coupled_jobs
            if done > 0 and done % jobs_of_half == 0:
                h = done // jobs_of_half - 1
                update(h)
                right_blocks(h)
                if h < halves - 1:
                    left_blocks(h)
    left_blocks(halves - 1)

    share = eig // n
    tiles_copy.wait()
    sends = []
    for h in range(halves):
        total = jnp.zeros((eig, LANES), F32)
        for t in range(tile_slots):
            kets[(h, t)].wait()
            product = jnp.dot(tiles_ref[t], ket_in[h, t], preferred_element_type=F32).astype(BF16)
            total = total + lax.dot_general(
                bras[t], product, (ROWS, ((), ())), preferred_element_type=F32
            )
        own[h] = total.reshape(n, share, LANES)
        dipole_out[h] = total.reshape(n, share, LANES).astype(BF16)
        for d in range(1, n):
            target = lax.rem(me + d, n)
            copy = pltpu.make_async_remote_copy(
                src_ref=dipole_out.at[h, target],
                dst_ref=dipole_in.at[h, d - 1],
                send_sem=dipole_send.at[h, d - 1],
                recv_sem=dipole_recv.at[h, d - 1],
                device_id=(sym, target),
                device_id_type=MESH,
            )
            copy.start()
            sends.append((h, d, copy))
    results = [own[h, me] for h in range(halves)]
    for h, d, copy in sends:
        copy.wait()
        results[h] = results[h] + dipole_in[h, d - 1].astype(F32)
    for h in range(halves):
        out_ref[0, :, h * LANES : (h + 1) * LANES] = results[h]


def on_device(
    n,
    syms,
    vectors,
    reflectors,
    factors,
    tiles,
    tile_left,
    tile_right,
    tile_occupied_mask,
    channels,
):
    start = vectors[0]
    panels = reflectors[0]
    rows, eig = start.shape
    count, width, _ = factors.shape[1:]
    tile_slots = tiles.shape[1]
    halves = eig // LANES
    phases = 2 * (n.bit_length() - 1)
    blocks = rows // BLOCK
    coupled_rows = count * (count - 1) // 2 * width
    reduced = coupled_rows + count * eig
    jobs = reduced // max(JOB_ROWS, 8 * n)
    share = eig // n
    dma = pltpu.SemaphoreType.DMA
    vmem = pl.BlockSpec(memory_space=pltpu.VMEM)
    smem = pl.BlockSpec(memory_space=pltpu.SMEM)
    hbm = pl.BlockSpec(memory_space=pl.ANY)
    return pl.pallas_call(
        functools.partial(kernel, n, syms),
        out_shape=jax.ShapeDtypeStruct((1, share, eig), F32),
        in_specs=[hbm, hbm, hbm, hbm, vmem, smem, smem, smem],
        out_specs=vmem,
        scratch_shapes=[
            pltpu.VMEM((blocks, BLOCK, eig), F32),
            pltpu.VMEM((blocks, BLOCK, count * width), F32),
            pltpu.VMEM((blocks, BLOCK, count * width), BF16),
            pltpu.VMEM((blocks, BLOCK, count * width), BF16),
            pltpu.VMEM((1, tile_slots), jnp.int32),
            pltpu.SMEM((1, tile_slots), jnp.int32),
            pltpu.VMEM((reduced, width), F32),
            pltpu.VMEM((reduced, width), F32),
            pltpu.VMEM((reduced, width), F32),
            pltpu.VMEM((count * width, count * width), F32),
            pltpu.VMEM((halves, count * width, LANES), BF16),
            pltpu.VMEM((halves, count * width, LANES), BF16),
            pltpu.VMEM((halves, tile_slots, BLOCK, LANES), BF16),
            pltpu.VMEM((halves, tile_slots, BLOCK, LANES), BF16),
            pltpu.VMEM((tile_slots, BLOCK, eig), BF16),
            pltpu.VMEM((halves, n, share, LANES), F32),
            pltpu.VMEM((halves, n, share, LANES), BF16),
            pltpu.VMEM((halves, n - 1, share, LANES), BF16),
            pltpu.VMEM((count, width, width), F32),
            pltpu.VMEM((tile_slots, BLOCK, BLOCK), BF16),
            dma((blocks,)),
            dma((blocks,)),
            dma((3,)),
            dma((2,)),
            dma((jobs, phases)),
            dma((jobs, phases)),
            dma((halves, tile_slots)),
            dma((halves, tile_slots)),
            dma((halves, n - 1)),
            dma((halves, n - 1)),
        ],
        compiler_params=pltpu.CompilerParams(
            collective_id=0, has_side_effects=True, vmem_limit_bytes=60 * 1024 * 1024
        ),
    )(
        start.reshape(blocks, BLOCK, eig),
        panels.reshape(blocks, BLOCK, count * width),
        factors[0],
        tiles[0],
        tile_right,
        tile_left,
        tile_occupied_mask,
        channels,
    )


def solution(mesh):
    return jax.shard_map(
        functools.partial(on_device, mesh.shape["row"], mesh.shape["sym"]),
        mesh=mesh,
        in_specs=(
            P("sym", "row", None),
            P("sym", "row", None),
            P("sym", None, None, None),
            P("sym", "row", None, None),
            P("sym", "row"),
            P("sym", "row"),
            P("sym", "row"),
            P("sym", "row"),
        ),
        out_specs=P("sym", "row", None),
        check_vma=False,
    )
```
